256 devices in a mesh: row: 16 (over y_hi, x, core), col: 16 (over z, y_lo).
Axes of the slice: x: 4, y: 4 (y_hi: 2, y_lo: 2; y = y_hi * 2 + y_lo), z: 8, core: 2. Of those that a mesh axis runs over, the one named last changes fastest.
Arguments:
- hessenberg: float32 [16384, 16384], P('row', 'col'), may hold values from -6 to 6, as said below
- factors: float32 [3, 32, 512, 512], P(None, 'row', 'col'), may hold values from -1 to 1, as said below
- active: int32 [3, 32], replicated, may hold values 0 or 1
Outputs:
- updated_slab: float32 [16384, 16384], P('row', 'col')
The draws below stay inside these ranges and needn't reach their ends.
Inputs may be any that keep to these rules, and one draw needn't show every extreme that they name: `hessenberg`: in global order, zero below the first subdiagonal. Each factors[f, s] is orthogonal up to float32 rounding.
All inputs are finite; a program needn't handle non-finite values.
Results may differ from the reference program's by a relative error of at most 0.0001.
Values sent between devices are 32-bit elements; how exact they have to be, the bound alone decides.
A program may use at most 64 MiB of HBM per device.

```python
import math
import jax
import jax.numpy as jnp
from jax import lax

ORDER = 16384
WIN = 512
PHASES = 3
NBLK = 32
N_ROW = 16
N_COL = 16


def draw_hessenberg(key, part):
    row_blocks = ORDER // WIN // N_ROW
    col_blocks = ORDER // WIN // N_COL
    values = jnp.clip(jax.random.normal(key, (ORDER, ORDER), jnp.float32), -6.0, 6.0)
    stored = jnp.arange(ORDER, dtype=jnp.int32)
    glob_row = (stored % (row_blocks * WIN) // WIN * N_ROW + stored // (row_blocks * WIN)) * WIN + stored % WIN
    glob_col = (stored % (col_blocks * WIN) // WIN * N_COL + stored // (col_blocks * WIN)) * WIN + stored % WIN
    return jnp.where(glob_row[:, None] <= glob_col[None, :] + 1, values, 0.0).astype(jnp.float32)


def draw_factors(key, part):
    spread = 0.3
    gaussian = jax.random.normal(key, (PHASES, ORDER // WIN, WIN, WIN), jnp.float32)
    unit_mat = jnp.eye(WIN, dtype=jnp.float32)
    iterate = (unit_mat + spread * gaussian / math.sqrt(WIN)) / 1.8
    for repeat in range(14):
        gram_mat = jnp.einsum('pkab,pkcb->pkac', iterate, iterate, precision=lax.Precision.HIGHEST)
        iterate = 1.5 * iterate - 0.5 * jnp.einsum('pkac,pkcb->pkab', gram_mat, iterate, precision=lax.Precision.HIGHEST)
    mirror = jax.random.normal(jax.random.fold_in(key, 7), (PHASES, ORDER // WIN, WIN), jnp.float32)
    mirror = mirror / jnp.sqrt(jnp.sum(mirror * mirror, axis=-1, keepdims=True))
    image = jnp.einsum('pkab,pkb->pka', iterate, mirror, precision=lax.Precision.HIGHEST)
    iterate = iterate - 2.0 * image[..., :, None] * mirror[..., None, :]
    return iterate.astype(jnp.float32)


def set_ends(array, rng, least, high):
    longest = array.shape.index(max(array.shape))
    spots = []
    for shift in (0, 1):
        where = [jax.random.randint(jax.random.fold_in(rng, axis), (), 0, length) for axis, length in enumerate(array.shape)]
        where[longest] = (where[longest] + shift) % array.shape[longest]
        spots.append(tuple(where))
    return array.at[spots[0]].set(least).at[spots[1]].set(high)


def setup_inputs(seed: int = 0) -> dict:
    arg_keys = jax.random.split(jax.random.key(seed), 4)
    return {
        "hessenberg": draw_hessenberg(jax.random.fold_in(arg_keys[3], 71), 0),
        "factors": draw_factors(jax.random.fold_in(arg_keys[3], 71), 0),
        "active": set_ends((jax.random.randint(arg_keys[2], (PHASES, NBLK), 0, 4) < 3).astype(jnp.int32), jax.random.fold_in(arg_keys[2], 1), 0, 1),
    }


PRECISE = lax.Precision.HIGHEST


def to_global(stored):
    row_blocks = NBLK // N_ROW
    col_blocks = NBLK // N_COL
    matrix = stored.reshape(N_ROW, row_blocks, WIN, ORDER).transpose(1, 0, 2, 3).reshape(ORDER, ORDER)
    return matrix.reshape(ORDER, N_COL, col_blocks, WIN).transpose(0, 2, 1, 3).reshape(ORDER, ORDER)


def to_stored(matrix):
    row_blocks = NBLK // N_ROW
    col_blocks = NBLK // N_COL
    stored = matrix.reshape(row_blocks, N_ROW, WIN, ORDER).transpose(1, 0, 2, 3).reshape(ORDER, ORDER)
    return stored.reshape(ORDER, col_blocks, N_COL, WIN).transpose(0, 2, 1, 3).reshape(ORDER, ORDER)


def reference(hessenberg, factors, active):
    row_blocks = NBLK // N_ROW
    matrix = to_global(hessenberg)
    natural = factors.reshape(PHASES, N_ROW, row_blocks, WIN, WIN).transpose(0, 2, 1, 3, 4).reshape(PHASES, NBLK, WIN, WIN)
    identity = jnp.eye(WIN, dtype=jnp.float32)
    indices = jnp.arange(ORDER, dtype=jnp.int32)
    for phase_idx in range(PHASES):
        offset = (phase_idx % 2) * (WIN // 2)
        win_count = NBLK - (phase_idx % 2)
        win_flags = active[phase_idx, :win_count]
        windows = jnp.where(win_flags[:, None, None] > 0, natural[phase_idx, :win_count], identity)
        slots = jnp.arange(win_count, dtype=jnp.int32)
        win_ends = offset + (slots + 1) * WIN
        window_rows = matrix[offset:offset + win_count * WIN].reshape(win_count, WIN, ORDER)
        updated = jnp.einsum("kab,kan->kbn", windows, window_rows, precision=PRECISE)
        keep_mask = indices[None, :] >= win_ends[:, None]
        window_rows = jnp.where(keep_mask[:, None, :], updated, window_rows)
        matrix = jnp.concatenate([matrix[:offset], window_rows.reshape(win_count * WIN, ORDER), matrix[offset + win_count * WIN:]], axis=0)
        win_starts = offset + slots * WIN
        window_cols = matrix[:, offset:offset + win_count * WIN].reshape(ORDER, win_count, WIN)
        updated = jnp.einsum("nka,kab->nkb", window_cols, windows, precision=PRECISE)
        keep_mask = indices[:, None] < win_starts[None, :]
        window_cols = jnp.where(keep_mask[:, :, None], updated, window_cols)
        matrix = jnp.concatenate([matrix[:, :offset], window_cols.reshape(ORDER, win_count * WIN), matrix[:, offset + win_count * WIN:]], axis=1)
    return to_stored(matrix)
```

```python
import functools

import jax
import jax.numpy as jnp
from jax import lax
from jax.experimental import pallas as pl
from jax.experimental.pallas import tpu as pltpu
from jax.sharding import PartitionSpec as P

MESH = pl.DeviceIdType.MESH
WIN = 512
HALF = 256
ROWS = 32
F32 = jnp.float32
BF16 = jnp.bfloat16
WINDOWS = ((0, 1), (0, 0), (1, 1))


def at(start, size):
    if isinstance(start, int):
        return pl.ds(start, size)
    return pl.ds(pl.multiple_of(start, size), size)


def unless(cond):
    return pl.when(jnp.logical_not(cond))


def kernel(
    flags, hess, fac, out,
    m1, m2, rf, cf, ta, s12, s21, s22, sh, zbuf, zhalf,
    lt_hi, lt_lo, r_hi, r_lo, w_hi, w_lo,
    ssem, rsem, lsem,
):
    r = lax.axis_index("row")
    c = lax.axis_index("col")
    core = r % 2
    x = (r // 2) % 4
    yh = r // 8
    yl = c % 2
    z = c // 2

    def row_of(xx):
        return yh * 8 + 2 * (xx % 4) + core

    xn, xp, xo = row_of(x + 1), row_of(x + 3), row_of(x + 2)
    zn, zp = (c + 2) % 16, (c + 14) % 16
    c_pair = c + 1 - 2 * yl
    r_pair = r + 1 - 2 * core
    r_far = (r + 8) % 16
    rm, rp = (r + 15) % 16, (r + 1) % 16
    cm, cp = (c + 15) % 16, (c + 1) % 16
    holder = yh == z // 4

    def scatter_target(xs):
        return (yh * 8 + 2 * x + yl, 2 * (4 * yh + xs) + core)

    def scatter_self(xs):
        return (core == yl) & (4 * yh + xs == z)

    bar = pltpu.get_barrier_semaphore()

    def greet(dev):
        pl.semaphore_signal(bar, inc=1, device_id=dev, device_id_type=MESH)

    for dev in (
        (r, c_pair), (r, zn), (r, zp), (r, cm), (r, cp),
        (r_pair, c), (r_far, c), (xn, c), (xp, c), (xo, c), (rm, c), (rp, c),
        (rm, cm), (rp, cp),
    ):
        greet(dev)
    for zz in range(8):
        own = (core == yl) & (zz == z)

        @pl.when(holder & jnp.logical_not(own))
        def _(zz=zz):
            greet((yh * 8 + 2 * x + yl, 2 * zz + core))

    self_target = holder & (core == yl)

    @pl.when(self_target)
    def _():
        pl.semaphore_wait(bar, 17)

    @unless(self_target)
    def _():
        pl.semaphore_wait(bar, 18)

    counts = [0, 0, 0]
    ends = []

    def take(which, n=1):
        first = counts[which]
        counts[which] += n
        return first

    def remote(src, dst, dev, cond=None):
        i = take(0)
        k = take(1)
        d = pltpu.make_async_remote_copy(
            src_ref=src, dst_ref=dst, send_sem=ssem.at[i], recv_sem=rsem.at[k],
            device_id=dev, device_id_type=MESH,
        )
        if cond is None:
            ends.append(d.wait_send)
        else:
            ends.append(lambda: pl.when(cond)(d.wait_send))
        return d

    def local(src, dst):
        i = take(2)
        return pltpu.make_async_copy(src, dst, lsem.at[i])

    load1 = local(hess, m1)
    load2 = local(hess, m2)
    load1.start()
    load2.start()

    def piece(f, q):
        return rf.at[f, :, at(q * ROWS, ROWS), :]

    def piece_k(f, k, q):
        return rf.at[f, k, at(q * ROWS, ROWS), :]

    def chunk(f, xx, kappa):
        return cf.at[f, xx // 2, :, kappa, xx % 2]

    def chunk_part(f, xx, kappa, part):
        return cf.at[f, xx // 2, pl.ds(4 * part, 4), kappa, xx % 2]

    dirs = (("p", zn, -1), ("m", zp, 1))
    Y, Z, A, B, G, C, own_rf, own_ta, own_cf = {}, {}, {}, {}, {}, {}, {}, {}, {}

    def own_sends(f):
        src = fac.at[f]
        Y[f] = remote(src, piece(f, c), (r, c_pair))
        Y[f].start()
        for name, dev, _ in dirs:
            Z[f, name, 0, 1] = remote(src, piece(f, c), (r, dev))
            Z[f, name, 0, 1].start()
        for d in (1, 2, 3):
            j = (x + d) % 4
            A[f, d] = remote(fac.at[f, j // 2, at((j % 2) * 16, 16), :], ta.at[f, x], (row_of(j), c))
            A[f, d].start()
        own_ta[f] = local(fac.at[f, x // 2, at((x % 2) * 16, 16), :], ta.at[f, x])
        own_ta[f].start()
        own_rf[f] = local(src, piece(f, c))
        own_rf[f].start()

    def pair_step(f):
        Y[f].wait_recv()
        for name, dev, _ in dirs:
            Z[f, name, 1, 1] = remote(piece(f, c_pair), piece(f, c_pair), (r, dev))
            Z[f, name, 1, 1].start()

    def z_step(f, hop):
        for s in (0, 1):
            for name, dev, sign in dirs:
                Z[f, name, s, hop].wait_recv()
                q = ((c if s == 0 else c_pair) + 2 * sign * hop + 16) % 16
                if hop < 3:
                    ref = piece(f, q)
                elif hop == 3:
                    ref = piece_k(f, 0 if name == "p" else 1, q)
                else:
                    continue
                Z[f, name, s, hop + 1] = remote(ref, ref, (r, dev))
                Z[f, name, s, hop + 1].start()

    def scatter_step(f):
        for d in (1, 2, 3):
            A[f, d].wait_recv()
        own_ta[f].wait()
        first = take(1, 8)
        own_cf[f] = local(ta.at[f, z % 4], cf.at[f, x // 2, z, yl, x % 2])
        for xs in range(4):
            i = take(0)
            d = pltpu.make_async_remote_copy(
                src_ref=ta.at[f, xs], dst_ref=cf.at[f, x // 2, z, yl, x % 2],
                send_sem=ssem.at[i], recv_sem=rsem.at[first + z],
                device_id=scatter_target(xs), device_id_type=MESH,
            )
            B[f, xs] = d
            unless(scatter_self(xs))(d.start)
            ends.append(lambda d=d, xs=xs: unless(scatter_self(xs))(d.wait_send))
        pl.when(self_target)(own_cf[f].start)
        B[f, "first"] = first

    def spread_step(f):
        first = B[f, "first"]
        mine = chunk(f, x, core)
        G[f, "far"] = remote(mine, mine, (r_far, c), holder)

        @pl.when(holder)
        def _():
            pl.when(self_target)(own_cf[f].wait)
            for zz in range(8):
                def arrived(zz=zz):
                    slot = cf.at[f, x // 2, zz, core, x % 2]
                    pltpu.make_async_remote_copy(
                        src_ref=slot, dst_ref=slot, send_sem=ssem.at[0], recv_sem=rsem.at[first + zz],
                        device_id=(r_far, c), device_id_type=MESH,
                    ).wait_recv()

                unless((core == yl) & (zz == z))(arrived)
            G[f, "far"].start()

        unless(holder)(G[f, "far"].wait_recv)
        for name, dev in (("p", xn), ("m", xp)):
            G[f, name, 1] = remote(mine, mine, (dev, c))
            G[f, name, 1].start()
        C[f, 0] = remote(mine, mine, (r_pair, c))
        C[f, 0].start()

    def x_step(f):
        for i, (name, dev, xs) in enumerate((("p", xn, (x + 3) % 4), ("m", xp, (x + 1) % 4))):
            G[f, name, 1].wait_recv()
            part = chunk_part(f, xs, core, i)
            G[f, name, 2] = remote(part, part, (dev, c))
            G[f, name, 2].start()
            got = chunk(f, xs, core)
            C[f, 1 + i] = remote(got, got, (r_pair, c))
            C[f, 1 + i].start()

    def x_last(f):
        for name in "pm":
            G[f, name, 2].wait_recv()
        got = chunk(f, (x + 2) % 4, core)
        C[f, 3] = remote(got, got, (r_pair, c))
        C[f, 3].start()

    def core_last(f):
        for i in range(4):
            C[f, i].wait_recv()
        own_rf[f].wait()

    def split(value):
        hi = value.astype(BF16)
        return hi, (value - hi.astype(F32)).astype(BF16)

    def dot(a, b):
        return jnp.dot(a, b, preferred_element_type=F32)

    def prepare(f):
        rows_i = lax.broadcasted_iota(jnp.int32, (WIN, WIN), 0)
        cols_i = lax.broadcasted_iota(jnp.int32, (WIN, WIN), 1)
        unit = (rows_i == cols_i).astype(F32)
        for k in range(2):
            on = jnp.full((WIN, WIN), flags[f, r + 16 * k], jnp.int32) > 0
            q = jnp.where(on, rf[f, k], unit)
            lt_hi[k], lt_lo[k] = split(q.T)
        for l in range(2):
            flag = flags[f, c + 16 * l]
            if f == 1 and l == 1:
                flag = flag * (c < 15).astype(jnp.int32)
            on = jnp.full((WIN, WIN), flag, jnp.int32) > 0
            q = jnp.where(on, cf[f, l].reshape(WIN, WIN), unit)
            r_hi[l], r_lo[l] = split(q)

    def right(rows, l):
        hi, lo = w_hi[0:rows], w_lo[0:rows]
        return dot(hi, r_hi[l]) + dot(hi, r_lo[l]) + dot(lo, r_hi[l])

    def both_sides(k, l):
        hi, lo = w_hi[...], w_lo[...]
        y = dot(lt_hi[k], hi) + dot(lt_hi[k], lo) + dot(lt_lo[k], hi)
        w_hi[...], w_lo[...] = split(y)
        return right(WIN, l)

    def above(k, l):
        return r + 16 * k < c + 16 * l

    def even_block(buf, k, l):
        @pl.when(above(k, l))
        def _():
            rs, cs = pl.ds(k * WIN, WIN), pl.ds(l * WIN, WIN)
            w_hi[...], w_lo[...] = split(buf[rs, cs])
            buf[rs, cs] = both_sides(k, l)

    l_wrap = (c == 0).astype(jnp.int32)
    k_wrap = (r == 0).astype(jnp.int32)
    l_over = (c == 15).astype(jnp.int32)
    k_over = (r == 15).astype(jnp.int32)

    def flip(slot, by):
        return slot + by * (1 - 2 * slot)

    def quad(buf, row, col):
        return buf.at[at(row, HALF), at(col, HALF)]

    def ends_before(dev_c, l):
        return dev_c + 16 * l < 31

    send, give_cond, take_cond, back = {}, {}, {}, {}

    def plan_out():
        for w, (k, l) in enumerate(WINDOWS):
            ks, ls = flip(k, k_wrap), flip(l, l_wrap)
            give_cond["12", w] = (r + 16 * k < cm + 16 * l) & ends_before(cm, l)
            give_cond["21", w] = rm + 16 * k < c + 16 * l
            give_cond["22", w] = (rm + 16 * k < cm + 16 * l) & ends_before(cm, l)
            take_cond["12", w] = above(k, l) & ends_before(c, l)
            take_cond["21", w] = above(k, l)
            take_cond["22", w] = take_cond["12", w]
            place = {
                "12": (k * WIN + HALF, ls * WIN, s12, (r, cm)),
                "21": (ks * WIN, l * WIN + HALF, s21, (rm, c)),
                "22": (ks * WIN, ls * WIN, s22, (rm, cm)),
            }
            for kind, (row, col, dst, dev) in place.items():
                send[kind, w] = remote(quad(m1, row, col), dst.at[w], dev, give_cond[kind, w])
        for l in range(2):
            give_cond["h", l] = (r == 0) & ends_before(cm, l)
            take_cond["h", l] = (r == 0) & ends_before(c, l)
            send["h", l] = remote(
                quad(m1, 0, flip(l, l_wrap) * WIN), sh.at[l], (r, cm), give_cond["h", l]
            )

    def give(kind, w, also=None):
        cond = give_cond[kind, w]
        pl.when(cond if also is None else cond & also)(send[kind, w].start)

    def got(kind, w):
        pl.when(take_cond[kind, w])(send[kind, w].wait_recv)

    def plan_back():
        for w, (k, l) in enumerate(WINDOWS):
            kr, lr = flip(k, k_over), flip(l, l_over)
            place = {
                "12": (0, HALF, k * WIN + HALF, lr * WIN, (r, cp)),
                "21": (HALF, 0, kr * WIN, l * WIN + HALF, (rp, c)),
                "22": (HALF, HALF, kr * WIN, lr * WIN, (rp, cp)),
            }
            for kind, (row, col, drow, dcol, dev) in place.items():
                src = zbuf.at[w, pl.ds(row, HALF), pl.ds(col, HALF)]
                back[kind, w] = remote(src, quad(m2, drow, dcol), dev, take_cond[kind, w])
        for l in range(2):
            back["h", l] = remote(
                zhalf.at[l, :, pl.ds(HALF, HALF)],
                quad(m2, 0, flip(l, l_over) * WIN), (r, cp), take_cond["h", l],
            )

    def odd_window(w):
        k, l = WINDOWS[w]
        for kind in ("12", "21", "22"):
            got(kind, w)

        @pl.when(above(k, l))
        def _():
            lo_half, hi_half = pl.ds(0, HALF), pl.ds(HALF, HALF)
            parts = (
                (lo_half, lo_half, m1[pl.ds(k * WIN + HALF, HALF), pl.ds(l * WIN + HALF, HALF)]),
                (lo_half, hi_half, s12[w]),
                (hi_half, lo_half, s21[w]),
                (hi_half, hi_half, s22[w]),
            )
            for rs, cs, value in parts:
                w_hi[rs, cs], w_lo[rs, cs] = split(value)
            result = both_sides(k, l)
            zbuf[w] = result
            m2[pl.ds(k * WIN + HALF, HALF), pl.ds(l * WIN + HALF, HALF)] = result[:HALF, :HALF]
            for kind in ("12", "21", "22"):
                pl.when(take_cond[kind, w])(back[kind, w].start)

    def top_window(l):
        got("h", l)

        @pl.when(take_cond["h", l])
        def _():
            top = pl.ds(0, HALF)
            w_hi[top, pl.ds(0, HALF)], w_lo[top, pl.ds(0, HALF)] = split(
                m1[top, pl.ds(l * WIN + HALF, HALF)]
            )
            w_hi[top, pl.ds(HALF, HALF)], w_lo[top, pl.ds(HALF, HALF)] = split(sh[l])
            result = right(HALF, l)
            zhalf[l] = result
            m2[top, pl.ds(l * WIN + HALF, HALF)] = result[:, :HALF]
            back["h", l].start()

    def unmoved():
        for k, l in WINDOWS:
            @pl.when(r + 16 * k + 1 == c + 16 * l)
            def _(k=k, l=l):
                rs, cs = pl.ds(k * WIN + HALF, HALF), pl.ds(l * WIN, HALF)
                m2[rs, cs] = m1[rs, cs]

        @pl.when((r == 0) & (c == 15))
        def _():
            rs, cs = pl.ds(0, HALF), pl.ds(WIN + HALF, HALF)
            m2[rs, cs] = m1[rs, cs]

    own_sends(0)
    plan_out()
    plan_back()

    @pl.when(c == 15)
    def _():
        for w in (0, 2):
            s12[w] = jnp.zeros((HALF, HALF), F32)
            s22[w] = jnp.zeros((HALF, HALF), F32)

    pair_step(0)
    scatter_step(0)
    z_step(0, 1)
    spread_step(0)
    own_sends(1)
    z_step(0, 2)
    x_step(0)
    z_step(0, 3)
    x_last(0)
    pair_step(1)
    scatter_step(1)
    z_step(0, 4)
    core_last(0)
    load1.wait()
    load2.wait()
    prepare(0)
    low = r > 0
    for l in range(2):
        pass
    even_block(m1, 0, 1)
    give("12", 0)
    give("21", 0, low)
    give("22", 0, low)
    z_step(1, 1)
    spread_step(1)
    even_block(m1, 0, 0)
    give("h", 0)
    give("h", 1)
    for kind in ("12", "21", "22"):
        give(kind, 1)
    z_step(1, 2)
    x_step(1)
    even_block(m1, 1, 1)
    give("21", 0, r == 0)
    give("22", 0, r == 0)
    for kind in ("12", "21", "22"):
        give(kind, 2)
    unmoved()
    own_sends(2)
    z_step(1, 3)
    x_last(1)
    z_step(1, 4)
    core_last(1)
    prepare(1)
    pair_step(2)
    scatter_step(2)
    odd_window(0)
    z_step(2, 1)
    spread_step(2)
    for l in range(2):
        top_window(l)
    odd_window(1)
    z_step(2, 2)
    x_step(2)
    odd_window(2)
    z_step(2, 3)
    x_last(2)
    z_step(2, 4)
    core_last(2)
    prepare(2)
    for key, cond in give_cond.items():
        pl.when(cond)(back[key].wait_recv)
    stores = []
    for k, l in ((1, 0),) + WINDOWS:
        if (k, l) != (1, 0):
            even_block(m2, k, l)
        rs, cs = pl.ds(k * WIN, WIN), pl.ds(l * WIN, WIN)
        d = local(m2.at[rs, cs], out.at[rs, cs])
        d.start()
        stores.append(d)
    for end in ends:
        end()
    for d in stores:
        d.wait()


def local(hessenberg, factors, active):
    sems = 150
    return pl.pallas_call(
        kernel,
        out_shape=jax.ShapeDtypeStruct(hessenberg.shape, F32),
        in_specs=[
            pl.BlockSpec(memory_space=pltpu.SMEM),
            pl.BlockSpec(memory_space=pl.ANY),
            pl.BlockSpec(memory_space=pl.ANY),
        ],
        out_specs=pl.BlockSpec(memory_space=pl.ANY),
        scratch_shapes=[
            pltpu.VMEM((1024, 1024), F32),
            pltpu.VMEM((1024, 1024), F32),
            pltpu.VMEM((3, 2, WIN, WIN), F32),
            pltpu.VMEM((3, 2, 8, 2, 2, 16, WIN), F32),
            pltpu.VMEM((3, 4, 16, WIN), F32),
            pltpu.VMEM((3, HALF, HALF), F32),
            pltpu.VMEM((3, HALF, HALF), F32),
            pltpu.VMEM((3, HALF, HALF), F32),
            pltpu.VMEM((2, HALF, HALF), F32),
            pltpu.VMEM((3, WIN, WIN), F32),
            pltpu.VMEM((2, HALF, WIN), F32),
            pltpu.VMEM((2, WIN, WIN), BF16),
            pltpu.VMEM((2, WIN, WIN), BF16),
            pltpu.VMEM((2, WIN, WIN), BF16),
            pltpu.VMEM((2, WIN, WIN), BF16),
            pltpu.VMEM((WIN, WIN), BF16),
            pltpu.VMEM((WIN, WIN), BF16),
            pltpu.SemaphoreType.DMA((sems,)),
            pltpu.SemaphoreType.DMA((sems,)),
            pltpu.SemaphoreType.DMA((16,)),
        ],
        compiler_params=pltpu.CompilerParams(
            collective_id=0, has_side_effects=True, vmem_limit_bytes=56 << 20
        ),
        name="sweep",
    )(active, hessenberg, factors)


def solution(mesh):
    return jax.shard_map(
        local,
        mesh=mesh,
        in_specs=(P("row", "col"), P(None, "row", "col", None), P()),
        out_specs=P("row", "col"),
        check_vma=False,
    )
```

```python
import functools

import jax
import jax.numpy as jnp
from jax import lax
from jax.experimental import pallas as pl
from jax.experimental.pallas import tpu as pltpu
from jax.sharding import PartitionSpec as P

MESH = pl.DeviceIdType.MESH
WIN = 512
HALF = 256
ROWS = 32
F32 = jnp.float32
BF16 = jnp.bfloat16
WINDOWS = ((0, 1), (0, 0), (1, 1))


PLAN = (
    ("cf", 0), ("y", 0), ("rf", 0), ("scatter", 0), ("y", 1), ("y", 2), ("cf", 1), ("cf", 2), ("pair", 0), ("far", 0),
    ("z", 0, 1), ("line", 0), ("z", 0, 2), ("x", 0), ("scatter", 1), ("z", 0, 3), ("xlast", 0), ("scatter", 2),
    ("z", 0, 4), ("far", 1), ("rf", 1), ("pair", 1),
    ("clear",), ("loaded",), ("pleft", 0), ("left0", 0), ("left0", 1), ("left0", 2), ("far", 2), ("pairlast", 0),
    ("pright", 0), ("block0", 0), ("block0", 1), ("block0", 2),
    ("z", 1, 1), ("line", 1), ("z", 1, 2), ("x", 1), ("z", 1, 3), ("xlast", 1), ("z", 1, 4), ("pairlast", 1),
    ("rf", 2), ("pair", 2), ("pleft", 1), ("pright", 1), ("odd", 0), ("top", 0), ("top", 1), ("odd", 1), ("odd", 2),
    ("z", 2, 1), ("line", 2), ("z", 2, 2), ("x", 2), ("z", 2, 3), ("xlast", 2), ("z", 2, 4), ("pairlast", 2),
    ("pleft", 2), ("pright", 2),
    ("returned",), ("block2", 1, 0), ("block2", 0, 1), ("block2", 0, 0), ("block2", 1, 1),
)


def at(start, size):
    if isinstance(start, int):
        return pl.ds(start, size)
    return pl.ds(pl.multiple_of(start, size), size)


def unless(cond):
    return pl.when(jnp.logical_not(cond))


def kernel(
    flags, hess, fac, out,
    m1, m2, rf, cf, ta, s12, s21, s22, sh, zbuf, zhalf,
    lt_hi, lt_lo, r_hi, r_lo, w_hi, w_lo, y_hi, y_lo,
    ssem, rsem, lsem,
):
    r = lax.axis_index("row")
    c = lax.axis_index("col")
    core = r % 2
    x = (r // 2) % 4
    yh = r // 8
    yl = c % 2
    z = c // 2

    def row_of(xx):
        return yh * 8 + 2 * (xx % 4) + core

    xn, xp = row_of(x + 1), row_of(x + 3)
    zn, zp = (c + 2) % 16, (c + 14) % 16
    c_pair = c + 1 - 2 * yl
    r_pair = r + 1 - 2 * core
    r_far = (r + 8) % 16
    rm, rp = (r + 15) % 16, (r + 1) % 16
    cm, cp = (c + 15) % 16, (c + 1) % 16
    spot = yh * 4 + x
    mirrored = core == yl

    def chip_row(t):
        return t // 4 * 8 + t % 4 * 2 + core

    def scatter_to(zz):
        return (yh * 8 + 2 * x + yl, 2 * zz + core)

    load1 = pltpu.make_async_copy(hess, m1, lsem.at[0])
    load2 = pltpu.make_async_copy(hess, m2, lsem.at[1])
    load1.start()
    load2.start()

    bar = pltpu.get_barrier_semaphore()

    def greet(dev):
        pl.semaphore_signal(bar, inc=1, device_id=dev, device_id_type=MESH)

    for dev in (
        (r, zn), (r, zp), (r, cm), (r, cp), (rm, c), (rp, c), (rm, cm), (rp, cp),
    ):
        greet(dev)
    for step in range(1, 8):
        greet((chip_row((spot + step) % 8), c))
    for zz in range(8):
        unless(mirrored & (zz == z))(functools.partial(greet, scatter_to(zz)))
    pl.when(mirrored)(lambda: pl.semaphore_wait(bar, 22))
    unless(mirrored)(lambda: pl.semaphore_wait(bar, 23))

    counts = [0, 0, 2]
    ends = []

    def take(which, n=1):
        first = counts[which]
        counts[which] += n
        return first

    def remote(src, dst, dev, cond=None):
        i = take(0)
        k = take(1)
        copy = pltpu.make_async_remote_copy(
            src_ref=src, dst_ref=dst, send_sem=ssem.at[i], recv_sem=rsem.at[k],
            device_id=dev, device_id_type=MESH,
        )
        if cond is None:
            ends.append(copy.wait_send)
        else:
            ends.append(lambda: pl.when(cond)(copy.wait_send))
        return copy

    def local(src, dst):
        i = take(2)
        return pltpu.make_async_copy(src, dst, lsem.at[i])

    def piece(f, q):
        return rf.at[f, :, at(q * ROWS, ROWS), :]

    def piece_k(f, k, q):
        return rf.at[f, k, at(q * ROWS, ROWS), :]

    def eighth(f, xx, kappa, e):
        return cf.at[f, xx // 2, :, kappa, xx % 2, e]

    def chunk(f, xx, kappa):
        return cf.at[f, xx // 2, :, kappa, xx % 2]

    def chunk_part(f, xx, kappa, part):
        return cf.at[f, xx // 2, pl.ds(4 * part, 4), kappa, xx % 2]

    dirs = (("p", zn, -1), ("m", zp, 1))
    Y, Z, A, B, G, C, own_rf, own_ta, own_cf = {}, {}, {}, {}, {}, {}, {}, {}, {}

    def own_pair(f):
        Y[f] = remote(fac.at[f], piece(f, c), (r, c_pair))
        Y[f].start()

    def own_row(f):
        src = fac.at[f]
        for name, dev, _ in dirs:
            Z[f, name, 0, 1] = remote(src, piece(f, c), (r, dev))
            Z[f, name, 0, 1].start()
        own_rf[f] = local(src, piece(f, c))
        own_rf[f].start()

    def own_col(f):
        def part(t):
            return fac.at[f, t % 4 // 2, at(t % 2 * 16 + t // 4 * 8, 8), :]

        for step in range(1, 8):
            t = (spot + step) % 8
            A[f, step] = remote(part(t), ta.at[f, spot], (chip_row(t), c))
            A[f, step].start()
        own_ta[f] = local(part(spot), ta.at[f, spot])
        own_ta[f].start()

    def pair_step(f):
        Y[f].wait_recv()
        own_rf[f].wait()
        for name, dev, _ in dirs:
            Z[f, name, 1, 1] = remote(piece(f, c_pair), piece(f, c_pair), (r, dev))
            Z[f, name, 1, 1].start()

    def z_step(f, hop):
        for s in (0, 1):
            for name, dev, sign in dirs:
                Z[f, name, s, hop].wait_recv()
                q = ((c if s == 0 else c_pair) + 2 * sign * hop + 16) % 16
                if hop < 3:
                    ref = piece(f, q)
                elif hop == 3:
                    ref = piece_k(f, 0 if name == "p" else 1, q)
                else:
                    continue
                Z[f, name, s, hop + 1] = remote(ref, ref, (r, dev))
                Z[f, name, s, hop + 1].start()

    def scatter_step(f):
        for step in range(1, 8):
            A[f, step].wait_recv()
        own_ta[f].wait()
        first = B[f] = take(1, 8)
        landing = eighth(f, x, yl, yh).at[z]
        own_cf[f] = local(ta.at[f, z], landing)
        for zz in range(8):
            copy = pltpu.make_async_remote_copy(
                src_ref=ta.at[f, zz], dst_ref=landing, send_sem=ssem.at[take(0)], recv_sem=rsem.at[first + z],
                device_id=scatter_to(zz), device_id_type=MESH,
            )
            home = mirrored & (zz == z)
            unless(home)(copy.start)
            ends.append(lambda copy=copy, home=home: unless(home)(copy.wait_send))
        pl.when(mirrored)(own_cf[f].start)

    def far_step(f):
        mine = eighth(f, x, core, yh)
        pl.when(mirrored)(own_cf[f].wait)
        for zz in range(8):
            slot = mine.at[zz]
            copy = pltpu.make_async_remote_copy(
                src_ref=slot, dst_ref=slot, send_sem=ssem.at[0], recv_sem=rsem.at[B[f] + zz],
                device_id=(r_far, c), device_id_type=MESH,
            )
            unless(mirrored & (zz == z))(copy.wait_recv)
        G[f, "far"] = remote(mine, mine, (r_far, c))
        G[f, "far"].start()

    def line_step(f):
        G[f, "far"].wait_recv()
        mine = chunk(f, x, core)
        for name, dev in (("p", xn), ("m", xp)):
            G[f, name, 1] = remote(mine, mine, (dev, c))
            G[f, name, 1].start()
        C[f, 0] = remote(mine, mine, (r_pair, c))
        C[f, 0].start()

    def x_step(f):
        for i, (name, dev, xs) in enumerate((("p", xn, (x + 3) % 4), ("m", xp, (x + 1) % 4))):
            G[f, name, 1].wait_recv()
            part = chunk_part(f, xs, core, i)
            G[f, name, 2] = remote(part, part, (dev, c))
            G[f, name, 2].start()
            got = chunk(f, xs, core)
            C[f, 1 + i] = remote(got, got, (r_pair, c))
            C[f, 1 + i].start()

    def x_last(f):
        for name in "pm":
            G[f, name, 2].wait_recv()
        got = chunk(f, (x + 2) % 4, core)
        C[f, 3] = remote(got, got, (r_pair, c))
        C[f, 3].start()

    def pair_last(f):
        for i in range(4):
            C[f, i].wait_recv()

    def split(value):
        hi = value.astype(BF16)
        return hi, (value - hi.astype(F32)).astype(BF16)

    def dot(a, b):
        return jnp.dot(a, b, preferred_element_type=F32)

    def unit():
        rows_i = lax.broadcasted_iota(jnp.int32, (WIN, WIN), 0)
        cols_i = lax.broadcasted_iota(jnp.int32, (WIN, WIN), 1)
        return (rows_i == cols_i).astype(F32)

    def prepare_left(f):
        for k in range(2):
            on = jnp.full((WIN, WIN), flags[f, r + 16 * k], jnp.int32) > 0
            lt_hi[k], lt_lo[k] = split(jnp.where(on, rf[f, k], unit()).T)

    def prepare_right(f):
        for l in range(2):
            flag = flags[f, c + 16 * l]
            if f == 1 and l == 1:
                flag = flag * (c < 15).astype(jnp.int32)
            on = jnp.full((WIN, WIN), flag, jnp.int32) > 0
            r_hi[l], r_lo[l] = split(jnp.where(on, cf[f, l].reshape(WIN, WIN), unit()))

    def times_right(hi, lo, l):
        return dot(hi, r_hi[l]) + dot(hi, r_lo[l]) + dot(lo, r_hi[l])

    def left(k, w):
        hi, lo = w_hi[...], w_lo[...]
        y_hi[w], y_lo[w] = split(dot(lt_hi[k], hi) + dot(lt_hi[k], lo) + dot(lt_lo[k], hi))

    def above(k, l):
        return r + 16 * k < c + 16 * l

    def place(w):
        k, l = WINDOWS[w]
        return pl.ds(k * WIN, WIN), pl.ds(l * WIN, WIN)

    def even_left(buf, w):
        k, l = WINDOWS[w]

        @pl.when(above(k, l))
        def _():
            w_hi[...], w_lo[...] = split(buf[place(w)])
            left(k, w)

    def even_right(buf, w):
        k, l = WINDOWS[w]

        @pl.when(above(k, l))
        def _():
            buf[place(w)] = times_right(y_hi[w], y_lo[w], l)

    l_wrap = (c == 0).astype(jnp.int32)
    k_wrap = (r == 0).astype(jnp.int32)
    l_over = (c == 15).astype(jnp.int32)
    k_over = (r == 15).astype(jnp.int32)

    def flip(slot, by):
        return slot + by * (1 - 2 * slot)

    def quad(buf, row, col):
        return buf.at[at(row, HALF), at(col, HALF)]

    def ends_before(dev_c, l):
        return dev_c + 16 * l < 31

    send, give_cond, take_cond, back = {}, {}, {}, {}

    def plan_out():
        for w, (k, l) in enumerate(WINDOWS):
            ks, ls = flip(k, k_wrap), flip(l, l_wrap)
            give_cond["12", w] = (r + 16 * k < cm + 16 * l) & ends_before(cm, l)
            give_cond["21", w] = rm + 16 * k < c + 16 * l
            give_cond["22", w] = (rm + 16 * k < cm + 16 * l) & ends_before(cm, l)
            take_cond["12", w] = above(k, l) & ends_before(c, l)
            take_cond["21", w] = above(k, l)
            take_cond["22", w] = take_cond["12", w]
            spots = {
                "12": (k * WIN + HALF, ls * WIN, s12, (r, cm)),
                "21": (ks * WIN, l * WIN + HALF, s21, (rm, c)),
                "22": (ks * WIN, ls * WIN, s22, (rm, cm)),
            }
            for kind, (row, col, dst, dev) in spots.items():
                send[kind, w] = remote(quad(m1, row, col), dst.at[w], dev, give_cond[kind, w])
        for l in range(2):
            give_cond["h", l] = (r == 0) & ends_before(cm, l)
            take_cond["h", l] = (r == 0) & ends_before(c, l)
            send["h", l] = remote(
                quad(m1, 0, flip(l, l_wrap) * WIN), sh.at[l], (r, cm), give_cond["h", l]
            )

    def give(kind, w, also=None):
        cond = give_cond[kind, w]
        pl.when(cond if also is None else cond & also)(send[kind, w].start)

    def got(kind, w):
        pl.when(take_cond[kind, w])(send[kind, w].wait_recv)

    def plan_back():
        for w, (k, l) in enumerate(WINDOWS):
            kr, lr = flip(k, k_over), flip(l, l_over)
            spots = {
                "12": (0, HALF, k * WIN + HALF, lr * WIN, (r, cp)),
                "21": (HALF, 0, kr * WIN, l * WIN + HALF, (rp, c)),
                "22": (HALF, HALF, kr * WIN, lr * WIN, (rp, cp)),
            }
            for kind, (row, col, drow, dcol, dev) in spots.items():
                src = zbuf.at[w, pl.ds(row, HALF), pl.ds(col, HALF)]
                back[kind, w] = remote(src, quad(m2, drow, dcol), dev, take_cond[kind, w])
        for l in range(2):
            back["h", l] = remote(
                zhalf.at[l, :, pl.ds(HALF, HALF)],
                quad(m2, 0, flip(l, l_over) * WIN), (r, cp), take_cond["h", l],
            )

    def odd_window(w):
        k, l = WINDOWS[w]
        for kind in ("12", "21", "22"):
            got(kind, w)

        @pl.when(above(k, l))
        def _():
            lo_half, hi_half = pl.ds(0, HALF), pl.ds(HALF, HALF)
            parts = (
                (lo_half, lo_half, m1[pl.ds(k * WIN + HALF, HALF), pl.ds(l * WIN + HALF, HALF)]),
                (lo_half, hi_half, s12[w]),
                (hi_half, lo_half, s21[w]),
                (hi_half, hi_half, s22[w]),
            )
            for rs, cs, value in parts:
                w_hi[rs, cs], w_lo[rs, cs] = split(value)
            left(k, w)
            result = times_right(y_hi[w], y_lo[w], l)
            zbuf[w] = result
            m2[pl.ds(k * WIN + HALF, HALF), pl.ds(l * WIN + HALF, HALF)] = result[:HALF, :HALF]
            for kind in ("12", "21", "22"):
                pl.when(take_cond[kind, w])(back[kind, w].start)

    def top_window(l):
        got("h", l)

        @pl.when(take_cond["h", l])
        def _():
            top = pl.ds(0, HALF)
            w_hi[top, pl.ds(0, HALF)], w_lo[top, pl.ds(0, HALF)] = split(
                m1[top, pl.ds(l * WIN + HALF, HALF)]
            )
            w_hi[top, pl.ds(HALF, HALF)], w_lo[top, pl.ds(HALF, HALF)] = split(sh[l])
            result = times_right(w_hi[top], w_lo[top], l)
            zhalf[l] = result
            m2[top, pl.ds(l * WIN + HALF, HALF)] = result[:, :HALF]
            back["h", l].start()

    def unmoved():
        for k, l in WINDOWS:
            @pl.when(r + 16 * k + 1 == c + 16 * l)
            def _(k=k, l=l):
                rs, cs = pl.ds(k * WIN + HALF, HALF), pl.ds(l * WIN, HALF)
                m2[rs, cs] = m1[rs, cs]

        @pl.when((r == 0) & (c == 15))
        def _():
            rs, cs = pl.ds(0, HALF), pl.ds(WIN + HALF, HALF)
            m2[rs, cs] = m1[rs, cs]

    plan_out()
    plan_back()

    def clear():
        @pl.when(c == 15)
        def _():
            for w in (0, 2):
                s12[w] = jnp.zeros((HALF, HALF), F32)
                s22[w] = jnp.zeros((HALF, HALF), F32)

    def loaded():
        load1.wait()
        load2.wait()

    def block0(w):
        even_right(m1, w)
        kinds = ("12", "21", "22")
        if w == 0:
            give("12", 0)
            give("21", 0, r > 0)
            give("22", 0, r > 0)
        elif w == 1:
            give("h", 0)
            give("h", 1)
            for kind in kinds:
                give(kind, 1)
        else:
            give("21", 0, r == 0)
            give("22", 0, r == 0)
            for kind in kinds:
                give(kind, 2)
            unmoved()

    def returned():
        for key, cond in give_cond.items():
            pl.when(cond)(back[key].wait_recv)

    stores = []

    def block2(k, l):
        if (k, l) in WINDOWS:
            even_left(m2, WINDOWS.index((k, l)))
            even_right(m2, WINDOWS.index((k, l)))
        rs, cs = pl.ds(k * WIN, WIN), pl.ds(l * WIN, WIN)
        copy = local(m2.at[rs, cs], out.at[rs, cs])
        copy.start()
        stores.append(copy)

    def left0(w):
        even_left(m1, w)

    steps = dict(
        y=own_pair, rf=own_row, cf=own_col, pair=pair_step, z=z_step, scatter=scatter_step, far=far_step, line=line_step, x=x_step,
        xlast=x_last, pairlast=pair_last, loaded=loaded, pleft=prepare_left,
        pright=prepare_right, left0=left0, block0=block0, clear=clear, odd=odd_window, top=top_window,
        returned=returned, block2=block2,
    )
    for name, *args in PLAN:
        steps[name](*args)
    for end in ends:
        end()
    for copy in stores:
        copy.wait()


def local(hessenberg, factors, active):
    sems = 160
    return pl.pallas_call(
        kernel,
        out_shape=jax.ShapeDtypeStruct(hessenberg.shape, F32),
        in_specs=[
            pl.BlockSpec(memory_space=pltpu.SMEM),
            pl.BlockSpec(memory_space=pl.ANY),
            pl.BlockSpec(memory_space=pl.ANY),
        ],
        out_specs=pl.BlockSpec(memory_space=pl.ANY),
        scratch_shapes=[
            pltpu.VMEM((1024, 1024), F32),
            pltpu.VMEM((1024, 1024), F32),
            pltpu.VMEM((3, 2, WIN, WIN), F32),
            pltpu.VMEM((3, 2, 8, 2, 2, 2, 8, WIN), F32),
            pltpu.VMEM((3, 8, 8, WIN), F32),
            pltpu.VMEM((3, HALF, HALF), F32),
            pltpu.VMEM((3, HALF, HALF), F32),
            pltpu.VMEM((3, HALF, HALF), F32),
            pltpu.VMEM((2, HALF, HALF), F32),
            pltpu.VMEM((3, WIN, WIN), F32),
            pltpu.VMEM((2, HALF, WIN), F32),
            pltpu.VMEM((2, WIN, WIN), BF16),
            pltpu.VMEM((2, WIN, WIN), BF16),
            pltpu.VMEM((2, WIN, WIN), BF16),
            pltpu.VMEM((2, WIN, WIN), BF16),
            pltpu.VMEM((WIN, WIN), BF16),
            pltpu.VMEM((WIN, WIN), BF16),
            pltpu.VMEM((3, WIN, WIN), BF16),
            pltpu.VMEM((3, WIN, WIN), BF16),
            pltpu.SemaphoreType.DMA((sems,)),
            pltpu.SemaphoreType.DMA((sems,)),
            pltpu.SemaphoreType.DMA((16,)),
        ],
        compiler_params=pltpu.CompilerParams(
            collective_id=0, has_side_effects=True, vmem_limit_bytes=56 << 20
        ),
        name="sweep",
    )(active, hessenberg, factors)


def solution(mesh):
    return jax.shard_map(
        local,
        mesh=mesh,
        in_specs=(P("row", "col"), P(None, "row", "col", None), P()),
        out_specs=P("row", "col"),
        check_vma=False,
    )
```

```python
import functools

import jax
import jax.numpy as jnp
from jax import lax
from jax.experimental import pallas as pl
from jax.experimental.pallas import tpu as pltpu
from jax.sharding import PartitionSpec as P

MESH = pl.DeviceIdType.MESH
WIN = 512
HALF = 256
ROWS = 32
F32 = jnp.float32
BF16 = jnp.bfloat16
WINDOWS = ((0, 1), (0, 0), (1, 1))


PLAN = (
    ("cf", 0), ("y", 0), ("rf", 0), ("scatter", 0), ("y", 1), ("y", 2), ("cf", 1), ("cf", 2), ("pair", 0),
    ("far", 0), ("z", 0, 1), ("line", 0), ("z", 0, 2), ("x", 0), ("scatter", 1), ("z", 0, 3), ("xlast", 0),
    ("scatter", 2), ("z", 0, 4), ("far", 1), ("clear",), ("loaded",), ("pleft", 0), ("left0", 0), ("left0", 1),
    ("left0", 2), ("far", 2), ("pairlast", 0), ("pright", 0), ("rf", 1), ("pair", 1), ("line", 1), ("block0", 0),
    ("block0", 1), ("block0", 2), ("z", 1, 1), ("z", 1, 2), ("x", 1), ("z", 1, 3), ("xlast", 1), ("z", 1, 4),
    ("pairlast", 1), ("rf", 2), ("pair", 2), ("pleft", 1), ("pright", 1), ("odd", 0), ("top", 0), ("top", 1),
    ("odd", 1), ("odd", 2), ("z", 2, 1), ("line", 2), ("z", 2, 2), ("x", 2), ("z", 2, 3), ("xlast", 2), ("z", 2, 4),
    ("pairlast", 2), ("pleft", 2), ("pright", 2), ("block2", 1, 0), ("returned", 0), ("block2", 0, 1),
    ("returned", 1), ("block2", 0, 0), ("returned", 2), ("block2", 1, 1),
)


def at(start, size):
    if isinstance(start, int):
        return pl.ds(start, size)
    return pl.ds(pl.multiple_of(start, size), size)


def unless(cond):
    return pl.when(jnp.logical_not(cond))


def kernel(
    flags, hess, fac, out,
    m1, m2, rf, cf, ta, s12, s21, s22, sh, zbuf, zhalf,
    lt_hi, lt_lo, r_hi, r_lo, w_hi, w_lo, y_hi, y_lo,
    ssem, rsem, lsem,
):
    r = lax.axis_index("row")
    c = lax.axis_index("col")
    core = r % 2
    x = (r // 2) % 4
    yh = r // 8
    yl = c % 2
    z = c // 2

    def row_of(xx):
        return yh * 8 + 2 * (xx % 4) + core

    xn, xp = row_of(x + 1), row_of(x + 3)
    zn, zp = (c + 2) % 16, (c + 14) % 16
    c_pair = c + 1 - 2 * yl
    r_pair = r + 1 - 2 * core
    r_far = (r + 8) % 16
    rm, rp = (r + 15) % 16, (r + 1) % 16
    cm, cp = (c + 15) % 16, (c + 1) % 16
    spot = yh * 4 + x
    mirrored = core == yl

    def chip_row(t):
        return t // 4 * 8 + t % 4 * 2 + core

    def scatter_to(zz):
        return (yh * 8 + 2 * x + yl, 2 * zz + core)

    load1 = pltpu.make_async_copy(hess, m1, lsem.at[0])
    load2 = pltpu.make_async_copy(hess, m2, lsem.at[1])
    load1.start()
    load2.start()

    bar = pltpu.get_barrier_semaphore()

    def greet(dev):
        pl.semaphore_signal(bar, inc=1, device_id=dev, device_id_type=MESH)

    for dev in (
        (r, zn), (r, zp), (r, cm), (r, cp), (rm, c), (rp, c), (rm, cm), (rp, cp),
    ):
        greet(dev)
    for step in range(1, 8):
        greet((chip_row((spot + step) % 8), c))
    for zz in range(8):
        unless(mirrored & (zz == z))(functools.partial(greet, scatter_to(zz)))
    pl.when(mirrored)(lambda: pl.semaphore_wait(bar, 22))
    unless(mirrored)(lambda: pl.semaphore_wait(bar, 23))

    counts = [0, 0, 2]
    ends = []

    def take(which, n=1):
        first = counts[which]
        counts[which] += n
        return first

    def remote(src, dst, dev, cond=None):
        i = take(0)
        k = take(1)
        copy = pltpu.make_async_remote_copy(
            src_ref=src, dst_ref=dst, send_sem=ssem.at[i], recv_sem=rsem.at[k],
            device_id=dev, device_id_type=MESH,
        )
        if cond is None:
            ends.append(copy.wait_send)
        else:
            ends.append(lambda: pl.when(cond)(copy.wait_send))
        return copy

    def local(src, dst):
        i = take(2)
        return pltpu.make_async_copy(src, dst, lsem.at[i])

    def piece(f, q):
        return rf.at[f, :, at(q * ROWS, ROWS), :]

    def piece_k(f, k, q):
        return rf.at[f, k, at(q * ROWS, ROWS), :]

    def eighth(f, xx, kappa, e):
        return cf.at[f, xx // 2, :, kappa, xx % 2, e]

    def chunk(f, xx, kappa):
        return cf.at[f, xx // 2, :, kappa, xx % 2]

    def chunk_part(f, xx, kappa, part):
        return cf.at[f, xx // 2, pl.ds(4 * part, 4), kappa, xx % 2]

    dirs = (("p", zn, -1), ("m", zp, 1))
    Y, Z, A, B, G, C, own_rf, own_ta, own_cf = {}, {}, {}, {}, {}, {}, {}, {}, {}

    def own_pair(f):
        Y[f] = remote(fac.at[f], piece(f, c), (r, c_pair))
        Y[f].start()

    def own_row(f):
        src = fac.at[f]
        for name, dev, _ in dirs:
            Z[f, name, 0, 1] = remote(src, piece(f, c), (r, dev))
            Z[f, name, 0, 1].start()
        own_rf[f] = local(src, piece(f, c))
        own_rf[f].start()

    def own_col(f):
        def part(t):
            return fac.at[f, t % 4 // 2, at(t % 2 * 16 + t // 4 * 8, 8), :]

        for step in range(1, 8):
            t = (spot + step) % 8
            A[f, step] = remote(part(t), ta.at[f, spot], (chip_row(t), c))
            A[f, step].start()
        own_ta[f] = local(part(spot), ta.at[f, spot])
        own_ta[f].start()

    def pair_step(f):
        Y[f].wait_recv()
        own_rf[f].wait()
        for name, dev, _ in dirs:
            Z[f, name, 1, 1] = remote(piece(f, c_pair), piece(f, c_pair), (r, dev))
            Z[f, name, 1, 1].start()

    def z_step(f, hop):
        for s in (0, 1):
            for name, dev, sign in dirs:
                Z[f, name, s, hop].wait_recv()
                q = ((c if s == 0 else c_pair) + 2 * sign * hop + 16) % 16
                if hop < 3:
                    ref = piece(f, q)
                elif hop == 3:
                    ref = piece_k(f, 0 if name == "p" else 1, q)
                else:
                    continue
                Z[f, name, s, hop + 1] = remote(ref, ref, (r, dev))
                Z[f, name, s, hop + 1].start()

    def scatter_step(f):
        for step in range(1, 8):
            A[f, step].wait_recv()
        own_ta[f].wait()
        first = B[f] = take(1, 8)
        landing = eighth(f, x, yl, yh).at[z]
        own_cf[f] = local(ta.at[f, z], landing)
        for zz in range(8):
            copy = pltpu.make_async_remote_copy(
                src_ref=ta.at[f, zz], dst_ref=landing, send_sem=ssem.at[take(0)], recv_sem=rsem.at[first + z],
                device_id=scatter_to(zz), device_id_type=MESH,
            )
            home = mirrored & (zz == z)
            unless(home)(copy.start)
            ends.append(lambda copy=copy, home=home: unless(home)(copy.wait_send))
        pl.when(mirrored)(own_cf[f].start)

    def far_step(f):
        mine = eighth(f, x, core, yh)
        pl.when(mirrored)(own_cf[f].wait)
        for zz in range(8):
            slot = mine.at[zz]
            copy = pltpu.make_async_remote_copy(
                src_ref=slot, dst_ref=slot, send_sem=ssem.at[0], recv_sem=rsem.at[B[f] + zz],
                device_id=(r_far, c), device_id_type=MESH,
            )
            unless(mirrored & (zz == z))(copy.wait_recv)
        G[f, "far"] = remote(mine, mine, (r_far, c))
        G[f, "far"].start()

    def line_step(f):
        G[f, "far"].wait_recv()
        mine = chunk(f, x, core)
        for name, dev in (("p", xn), ("m", xp)):
            G[f, name, 1] = remote(mine, mine, (dev, c))
            G[f, name, 1].start()
        C[f, 0] = remote(mine, mine, (r_pair, c))
        C[f, 0].start()

    def x_step(f):
        for i, (name, dev, xs) in enumerate((("p", xn, (x + 3) % 4), ("m", xp, (x + 1) % 4))):
            G[f, name, 1].wait_recv()
            part = chunk_part(f, xs, core, i)
            G[f, name, 2] = remote(part, part, (dev, c))
            G[f, name, 2].start()
            got = chunk(f, xs, core)
            C[f, 1 + i] = remote(got, got, (r_pair, c))
            C[f, 1 + i].start()

    def x_last(f):
        for name in "pm":
            G[f, name, 2].wait_recv()
        got = chunk(f, (x + 2) % 4, core)
        C[f, 3] = remote(got, got, (r_pair, c))
        C[f, 3].start()

    def pair_last(f):
        for i in range(4):
            C[f, i].wait_recv()

    def split(value):
        hi = value.astype(BF16)
        return hi, (value - hi.astype(F32)).astype(BF16)

    def dot(a, b):
        return jnp.dot(a, b, preferred_element_type=F32)

    def unit():
        rows_i = lax.broadcasted_iota(jnp.int32, (WIN, WIN), 0)
        cols_i = lax.broadcasted_iota(jnp.int32, (WIN, WIN), 1)
        return (rows_i == cols_i).astype(F32)

    def prepare_left(f):
        for k in range(2):
            on = jnp.full((WIN, WIN), flags[f, r + 16 * k], jnp.int32) > 0
            lt_hi[k], lt_lo[k] = split(jnp.where(on, rf[f, k], unit()).T)

    def prepare_right(f):
        for l in range(2):
            flag = flags[f, c + 16 * l]
            if f == 1 and l == 1:
                flag = flag * (c < 15).astype(jnp.int32)
            on = jnp.full((WIN, WIN), flag, jnp.int32) > 0
            r_hi[l], r_lo[l] = split(jnp.where(on, cf[f, l].reshape(WIN, WIN), unit()))

    def times_right(hi, lo, l):
        return dot(hi, r_hi[l]) + dot(hi, r_lo[l]) + dot(lo, r_hi[l])

    def left(k, w):
        hi, lo = w_hi[...], w_lo[...]
        y_hi[w], y_lo[w] = split(dot(lt_hi[k], hi) + dot(lt_hi[k], lo) + dot(lt_lo[k], hi))

    def above(k, l):
        return r + 16 * k < c + 16 * l

    def place(w):
        k, l = WINDOWS[w]
        return pl.ds(k * WIN, WIN), pl.ds(l * WIN, WIN)

    def even_left(buf, w):
        k, l = WINDOWS[w]

        @pl.when(above(k, l))
        def _():
            w_hi[...], w_lo[...] = split(buf[place(w)])
            left(k, w)

    def even_right(buf, w):
        k, l = WINDOWS[w]

        @pl.when(above(k, l))
        def _():
            buf[place(w)] = times_right(y_hi[w], y_lo[w], l)

    l_wrap = (c == 0).astype(jnp.int32)
    k_wrap = (r == 0).astype(jnp.int32)
    l_over = (c == 15).astype(jnp.int32)
    k_over = (r == 15).astype(jnp.int32)

    def flip(slot, by):
        return slot + by * (1 - 2 * slot)

    def quad(buf, row, col):
        return buf.at[at(row, HALF), at(col, HALF)]

    def ends_before(dev_c, l):
        return dev_c + 16 * l < 31

    send, give_cond, take_cond, back = {}, {}, {}, {}

    def plan_out():
        for w, (k, l) in enumerate(WINDOWS):
            ks, ls = flip(k, k_wrap), flip(l, l_wrap)
            give_cond["12", w] = (r + 16 * k < cm + 16 * l) & ends_before(cm, l)
            give_cond["21", w] = rm + 16 * k < c + 16 * l
            give_cond["22", w] = (rm + 16 * k < cm + 16 * l) & ends_before(cm, l)
            take_cond["12", w] = above(k, l) & ends_before(c, l)
            take_cond["21", w] = above(k, l)
            take_cond["22", w] = take_cond["12", w]
            spots = {
                "12": (k * WIN + HALF, ls * WIN, s12, (r, cm)),
                "21": (ks * WIN, l * WIN + HALF, s21, (rm, c)),
                "22": (ks * WIN, ls * WIN, s22, (rm, cm)),
            }
            for kind, (row, col, dst, dev) in spots.items():
                send[kind, w] = remote(quad(m1, row, col), dst.at[w], dev, give_cond[kind, w])
        for l in range(2):
            give_cond["h", l] = (r == 0) & ends_before(cm, l)
            take_cond["h", l] = (r == 0) & ends_before(c, l)
            send["h", l] = remote(
                quad(m1, 0, flip(l, l_wrap) * WIN), sh.at[l], (r, cm), give_cond["h", l]
            )

    def give(kind, w, also=None):
        cond = give_cond[kind, w]
        pl.when(cond if also is None else cond & also)(send[kind, w].start)

    def got(kind, w):
        pl.when(take_cond[kind, w])(send[kind, w].wait_recv)

    def plan_back():
        for w, (k, l) in enumerate(WINDOWS):
            kr, lr = flip(k, k_over), flip(l, l_over)
            spots = {
                "12": (0, HALF, k * WIN + HALF, lr * WIN, (r, cp)),
                "21": (HALF, 0, kr * WIN, l * WIN + HALF, (rp, c)),
                "22": (HALF, HALF, kr * WIN, lr * WIN, (rp, cp)),
            }
            for kind, (row, col, drow, dcol, dev) in spots.items():
                src = zbuf.at[w, pl.ds(row, HALF), pl.ds(col, HALF)]
                back[kind, w] = remote(src, quad(m2, drow, dcol), dev, take_cond[kind, w])
        for l in range(2):
            back["h", l] = remote(
                zhalf.at[l, :, pl.ds(HALF, HALF)],
                quad(m2, 0, flip(l, l_over) * WIN), (r, cp), take_cond["h", l],
            )

    def odd_window(w):
        k, l = WINDOWS[w]
        for kind in ("12", "21", "22"):
            got(kind, w)

        @pl.when(above(k, l))
        def _():
            lo_half, hi_half = pl.ds(0, HALF), pl.ds(HALF, HALF)
            parts = (
                (lo_half, lo_half, m1[pl.ds(k * WIN + HALF, HALF), pl.ds(l * WIN + HALF, HALF)]),
                (lo_half, hi_half, s12[w]),
                (hi_half, lo_half, s21[w]),
                (hi_half, hi_half, s22[w]),
            )
            for rs, cs, value in parts:
                w_hi[rs, cs], w_lo[rs, cs] = split(value)
            left(k, w)
            result = times_right(y_hi[w], y_lo[w], l)
            zbuf[w] = result
            m2[pl.ds(k * WIN + HALF, HALF), pl.ds(l * WIN + HALF, HALF)] = result[:HALF, :HALF]
            for kind in ("12", "21", "22"):
                pl.when(take_cond[kind, w])(back[kind, w].start)

    def top_window(l):
        got("h", l)

        @pl.when(take_cond["h", l])
        def _():
            top = pl.ds(0, HALF)
            w_hi[top, pl.ds(0, HALF)], w_lo[top, pl.ds(0, HALF)] = split(
                m1[top, pl.ds(l * WIN + HALF, HALF)]
            )
            w_hi[top, pl.ds(HALF, HALF)], w_lo[top, pl.ds(HALF, HALF)] = split(sh[l])
            result = times_right(w_hi[top], w_lo[top], l)
            zhalf[l] = result
            m2[top, pl.ds(l * WIN + HALF, HALF)] = result[:, :HALF]
            back["h", l].start()

    def unmoved():
        for k, l in WINDOWS:
            @pl.when(r + 16 * k + 1 == c + 16 * l)
            def _(k=k, l=l):
                rs, cs = pl.ds(k * WIN + HALF, HALF), pl.ds(l * WIN, HALF)
                m2[rs, cs] = m1[rs, cs]

        @pl.when((r == 0) & (c == 15))
        def _():
            rs, cs = pl.ds(0, HALF), pl.ds(WIN + HALF, HALF)
            m2[rs, cs] = m1[rs, cs]

    plan_out()
    plan_back()

    def clear():
        @pl.when(c == 15)
        def _():
            for w in (0, 2):
                s12[w] = jnp.zeros((HALF, HALF), F32)
                s22[w] = jnp.zeros((HALF, HALF), F32)

    def loaded():
        load1.wait()
        load2.wait()

    def block0(w):
        even_right(m1, w)
        kinds = ("12", "21", "22")
        if w == 0:
            give("12", 0)
            give("21", 0, r > 0)
            give("22", 0, r > 0)
        elif w == 1:
            give("h", 0)
            give("h", 1)
            for kind in kinds:
                give(kind, 1)
        else:
            give("21", 0, r == 0)
            give("22", 0, r == 0)
            for kind in kinds:
                give(kind, 2)
            unmoved()

    def returned(w):
        def arrive(key, cond):
            pl.when(cond)(back[key].wait_recv)

        for kind in ("12", "21", "22"):
            key = kind, w
            if w == 1 and kind != "21":
                arrive(key, give_cond[key] & (c > 0))
            else:
                arrive(key, give_cond[key])
            if w == 0 and kind != "21":
                arrive((kind, 1), give_cond[kind, 1] & (c == 0))
        if w == 0:
            for l in range(2):
                arrive(("h", l), give_cond["h", l])

    stores = []

    def block2(k, l):
        if (k, l) in WINDOWS:
            even_left(m2, WINDOWS.index((k, l)))
            even_right(m2, WINDOWS.index((k, l)))
        rs, cs = pl.ds(k * WIN, WIN), pl.ds(l * WIN, WIN)
        copy = local(m2.at[rs, cs], out.at[rs, cs])
        copy.start()
        stores.append(copy)

    def left0(w):
        even_left(m1, w)

    steps = dict(
        y=own_pair, rf=own_row, cf=own_col, pair=pair_step, z=z_step, scatter=scatter_step, far=far_step, line=line_step, x=x_step,
        xlast=x_last, pairlast=pair_last, loaded=loaded, pleft=prepare_left,
        pright=prepare_right, left0=left0, block0=block0, clear=clear, odd=odd_window, top=top_window,
        returned=returned, block2=block2,
    )
    for name, *args in PLAN:
        steps[name](*args)
    for end in ends:
        end()
    for copy in stores:
        copy.wait()


def local(hessenberg, factors, active):
    sems = 160
    return pl.pallas_call(
        kernel,
        out_shape=jax.ShapeDtypeStruct(hessenberg.shape, F32),
        in_specs=[
            pl.BlockSpec(memory_space=pltpu.SMEM),
            pl.BlockSpec(memory_space=pl.ANY),
            pl.BlockSpec(memory_space=pl.ANY),
        ],
        out_specs=pl.BlockSpec(memory_space=pl.ANY),
        scratch_shapes=[
            pltpu.VMEM((1024, 1024), F32),
            pltpu.VMEM((1024, 1024), F32),
            pltpu.VMEM((3, 2, WIN, WIN), F32),
            pltpu.VMEM((3, 2, 8, 2, 2, 2, 8, WIN), F32),
            pltpu.VMEM((3, 8, 8, WIN), F32),
            pltpu.VMEM((3, HALF, HALF), F32),
            pltpu.VMEM((3, HALF, HALF), F32),
            pltpu.VMEM((3, HALF, HALF), F32),
            pltpu.VMEM((2, HALF, HALF), F32),
            pltpu.VMEM((3, WIN, WIN), F32),
            pltpu.VMEM((2, HALF, WIN), F32),
            pltpu.VMEM((2, WIN, WIN), BF16),
            pltpu.VMEM((2, WIN, WIN), BF16),
            pltpu.VMEM((2, WIN, WIN), BF16),
            pltpu.VMEM((2, WIN, WIN), BF16),
            pltpu.VMEM((WIN, WIN), BF16),
            pltpu.VMEM((WIN, WIN), BF16),
            pltpu.VMEM((3, WIN, WIN), BF16),
            pltpu.VMEM((3, WIN, WIN), BF16),
            pltpu.SemaphoreType.DMA((sems,)),
            pltpu.SemaphoreType.DMA((sems,)),
            pltpu.SemaphoreType.DMA((16,)),
        ],
        compiler_params=pltpu.CompilerParams(
            collective_id=0, has_side_effects=True, vmem_limit_bytes=56 << 20
        ),
        name="sweep",
    )(active, hessenberg, factors)


def solution(mesh):
    return jax.shard_map(
        local,
        mesh=mesh,
        in_specs=(P("row", "col"), P(None, "row", "col", None), P()),
        out_specs=P("row", "col"),
        check_vma=False,
    )
```
